512 devices in a mesh: pts: 32 (over z_lo, y, core), ctr: 16 (over z_hi, x).
Axes of the slice: x: 4, y: 8, z: 8 (z_hi: 4, z_lo: 2; z = z_hi * 2 + z_lo), core: 2. Of those that a mesh axis runs over, the one named last changes fastest.
Arguments:
- points: bfloat16 [8192, 256], P('pts', 'ctr'), may hold values from -6 to 6
- centres: bfloat16 [8192, 256], P('ctr', 'pts'), may hold values from -6 to 6
- precisions: float32 [256], replicated, may hold values from 9.765625e-05 to 0.01953125
- targets: bfloat16 [8192, 128], P('pts', 'ctr'), may hold values from -6 to 6
Outputs:
- coefficients: float32 [8192, 128], P('ctr')
- residual: float32 [8192, 128], P('ctr')
The draws below stay inside these ranges and needn't reach their ends.
All inputs are finite; a program needn't handle non-finite values.
Results may differ from the reference program's by a relative error of at most 0.0033.
Values may be sent and summed in bfloat16 or wider, within the bound.
No kernel may reach another device: no remote copies, remote signals or barrier semaphores. Data moves between devices by JAX's collectives and lax.ppermute only.
A program may use at most 64 MiB of HBM per device.

```python
import math
import jax
import jax.numpy as jnp
from jax import lax

FEATURES = 256
TARGETS = 128
BLOCK = 512
POINTS_DEV = 256
NEWTON = 2
ITERS = 1
CENTRES_DEV = 512
POINTS = 8192
CENTRES = 8192
N_PTS = 32
N_CTR = 16


def steps_of(stream_key, shape, split, smallest, top_value):
    def one(axis_at, shards_of):
        draws = jax.random.uniform(jax.random.fold_in(jax.random.fold_in(stream_key, 6), axis_at), (shards_of,), jnp.float32, smallest / len(split), top_value / len(split))
        return jnp.repeat(jnp.exp(draws), shape[axis_at] // shards_of).reshape((-1,) + (1,) * (len(shape) - axis_at - 1))

    factor_of = one(*split[0])
    for cut in split[1:]:
        factor_of = factor_of * one(*cut)
    return factor_of


def bell_draw(rng, extent, scale, bound, shards=(), kind=jnp.bfloat16):
    array = scale * jax.random.normal(rng, extent, jnp.float32)
    if shards:
        array = array * steps_of(rng, extent, shards, -0.22, 0.18)
    return jnp.clip(array, -bound, bound).astype(kind)


def setup_inputs(seed: int = 0) -> dict:
    keys = jax.random.split(jax.random.key(seed), 5)
    points = bell_draw(keys[0], (POINTS, FEATURES), 1.0, 6.0, ((0, 32), (1, 16)))
    centres = bell_draw(keys[1], (CENTRES, FEATURES), 1.0, 6.0, ((0, 16), (1, 32)))
    precisions = jnp.clip(jnp.exp(jax.random.uniform(keys[2], (FEATURES,), jnp.float32, math.log(9.765625145519152e-05), math.log(0.01953125))), 9.765625145519152e-05, 0.01953125)
    targets = bell_draw(keys[3], (POINTS, TARGETS), 1.0, 6.0, ((0, 32), (1, 16)))
    return dict(points=points, centres=centres, precisions=precisions, targets=targets)


ridge_weight = 0.05
jitter_term = 0.1
highest = lax.Precision.HIGHEST

def block_product(matrices, vectors):
    grouped = vectors.reshape(matrices.shape[0], matrices.shape[1], vectors.shape[1])
    return jnp.einsum('bij,bjr->bir', matrices, grouped, precision=highest).reshape(vectors.shape)

def batched(left, right):
    return jnp.einsum('bij,bjk->bik', left, right, precision=highest)

def reference(points, centres, precisions, targets):
    total = POINTS_DEV * N_PTS
    count_blocks = CENTRES_DEV * N_CTR // BLOCK
    centre_float = centres.astype(jnp.float32)
    centre_square = lax.optimization_barrier(jnp.sum(precisions * centre_float * centre_float, axis=1))
    point_float = points.astype(jnp.float32)
    point_square = lax.optimization_barrier(jnp.sum(precisions * point_float * point_float, axis=1))
    scaled_points = (point_float * precisions).astype(jnp.bfloat16)
    scaled_centres = (centre_float * precisions).astype(jnp.bfloat16)
    grouped_scaled = scaled_centres.astype(jnp.float32).reshape(count_blocks, BLOCK, FEATURES)
    grouped_centres = centre_float.reshape(count_blocks, BLOCK, FEATURES)
    block_cross = jnp.einsum('bif,bjf->bij', grouped_scaled, grouped_centres, precision=highest)
    grouped_square = centre_square.reshape(count_blocks, BLOCK)
    similar = jnp.exp(-(grouped_square[:, :, None] + grouped_square[:, None, :] - 2.0 * block_cross))
    identity = jnp.eye(BLOCK, dtype=jnp.float32)
    blocks = 0.5 * (similar + jnp.swapaxes(similar, 1, 2)) + jitter_term * identity
    scale = jnp.sqrt(lax.optimization_barrier(jnp.sum(blocks * blocks, axis=(1, 2))))
    current_y = blocks / scale[:, None, None]
    current_z = jnp.broadcast_to(identity, blocks.shape)
    for newton_step in range(NEWTON):
        factor = 3.0 * identity - batched(current_z, current_y)
        current_y, current_z = (0.5 * batched(current_y, factor), 0.5 * batched(current_z, factor))
    root = current_z
    row_scaled = scaled_points.reshape(N_PTS, POINTS_DEV, FEATURES)
    row_square = point_square.reshape(N_PTS, POINTS_DEV)
    row_targets = targets.astype(jnp.float32).reshape(N_PTS, POINTS_DEV, TARGETS)

    def kernel_rows(scaled_block, square_block):
        cross_term = jnp.dot(scaled_block, centres.T, preferred_element_type=jnp.float32)
        return jnp.exp(-(square_block[:, None] + centre_square[None, :] - 2.0 * cross_term))

    def right_step(accumulated, inputs):
        scaled_block, square_block, target_block = inputs
        kernel_block = kernel_rows(scaled_block, square_block)
        term = lax.dot_general(kernel_block, target_block, (((0,), (0,)), ((), ())), precision=highest)
        return (accumulated + term, None)
    zeros = jnp.zeros((CENTRES_DEV * N_CTR, TARGETS), jnp.float32)
    right, _ = lax.scan(right_step, zeros, (row_scaled, row_square, row_targets))
    right = right / math.sqrt(total)

    def normal_apply(vector):

        def normal_step(accumulated, inputs):
            scaled_block, square_block = inputs
            kernel_block = kernel_rows(scaled_block, square_block)
            values = jnp.dot(kernel_block, vector, precision=highest)
            term = lax.dot_general(kernel_block, values, (((0,), (0,)), ((), ())), precision=highest)
            return (accumulated + term, None)
        gathered, _ = lax.scan(normal_step, zeros, (row_scaled, row_square))
        return gathered / total + ridge_weight * block_product(blocks, vector)

    def operator(vector):
        return block_product(root, normal_apply(block_product(root, vector)))
    gradient = block_product(root, right)
    solution = jnp.zeros_like(gradient)
    residual = gradient
    direction = gradient
    norm_now = lax.optimization_barrier(jnp.sum(residual * residual, axis=0))
    for iteration in range(ITERS):
        image = operator(direction)
        step_size = norm_now / lax.optimization_barrier(jnp.sum(direction * image, axis=0))
        solution = solution + step_size * direction
        residual = residual - step_size * image
        norm_next = lax.optimization_barrier(jnp.sum(residual * residual, axis=0))
        direction = residual + norm_next / norm_now * direction
        norm_now = norm_next
    return (block_product(root, solution), residual)
```

```python
import math

import jax
import jax.numpy as jnp
from jax import lax
from jax.sharding import PartitionSpec as P

BLOCK = 512
ridge_weight = 0.05
jitter_term = 0.1
f32, bf16 = jnp.float32, jnp.bfloat16
highest = lax.Precision.HIGHEST
high = lax.Precision.HIGH


def dot(left, right, dims, precision=highest):
    return lax.dot_general(
        left, right, (dims, ((), ())), precision=precision, preferred_element_type=f32
    )


def gather(part, axis, count):
    return lax.all_to_all(jnp.broadcast_to(part[None], (count,) + part.shape), axis, 0, 0)


def scatter_sum(parts, axis):
    return jnp.sum(lax.all_to_all(parts, axis, 0, 0).astype(f32), axis=0)


def split(value):
    first = value.astype(bf16)
    rest = value - first.astype(f32)
    second = rest.astype(bf16)
    return first, second, (rest - second.astype(f32)).astype(bf16)


def on_device(points, centres, precisions, targets):
    n_pts, n_ctr = lax.axis_size("pts"), lax.axis_size("ctr")
    rows, cols = points.shape[0], centres.shape[0]
    width = targets.shape[1] * n_ctr
    total = rows * n_pts
    feats = points.shape[1]

    own_centres = centres.T
    centres_t = gather(own_centres, "pts", n_pts).reshape(-1, cols)
    own_points = jnp.concatenate([points.T, targets.T], axis=0)
    both = gather(own_points, "ctr", n_ctr)
    points_t = both[:, :feats].reshape(-1, rows)
    targets_t = both[:, feats:].reshape(-1, rows)

    weight = precisions[:, None]
    centre_float = centres_t.astype(f32)
    centre_square = jnp.sum(weight * centre_float * centre_float, axis=0)
    scaled_centres = (centre_float * weight).astype(bf16)
    point_float = points_t.astype(f32)
    point_square = jnp.sum(weight * point_float * point_float, axis=0)
    scaled_points = (point_float * weight).astype(bf16)

    cross_term = dot(scaled_points, centres_t, ((0,), (0,)), None)
    kernel_tile = jnp.exp(-(point_square[:, None] + centre_square[None, :] - 2.0 * cross_term))

    right_part = dot(kernel_tile, targets_t.astype(f32), ((0,), (1,)))
    right_own = scatter_sum(right_part.reshape(n_pts, cols // n_pts, width), "pts")

    block_cross = dot(scaled_centres, centres_t, ((0,), (0,)), None)
    similar = jnp.exp(-(centre_square[:, None] + centre_square[None, :] - 2.0 * block_cross))
    identity = jnp.eye(BLOCK, dtype=f32)
    blocks = 0.5 * (similar + similar.T) + jitter_term * identity
    scale = jnp.sqrt(jnp.sum(blocks * blocks))
    first = blocks / scale
    second = dot(first, first, ((1,), (0,)))
    inner = 0.0625 * second - 0.5625 * first
    root = (
        2.25 * identity
        - 2.4375 * first
        + 1.6875 * second
        + dot(second, inner, ((1,), (0,)))
    )

    right = gather(right_own, "pts", n_pts).reshape(cols, width) / math.sqrt(total)
    gradient = dot(root, right, ((1,), (0,)))
    spread = dot(root, gradient, ((1,), (0,)))
    damped = ridge_weight * dot(blocks, spread, ((1,), (0,)))
    norm_part = jnp.sum(gradient * gradient, axis=0)
    curve_part = jnp.sum(spread * damped, axis=0)

    value_part = dot(kernel_tile, spread, ((1,), (0,))).astype(bf16)
    value_own = scatter_sum(value_part.reshape(n_ctr, rows // n_ctr, width), "ctr")
    sums = jnp.stack(split(norm_part) + split(curve_part))
    sums = jnp.pad(sums, ((0, rows // n_ctr - sums.shape[0]), (0, 0)))
    value_all = gather(jnp.concatenate([value_own.astype(bf16), sums], axis=0), "ctr", n_ctr)
    values = value_all[:, : rows // n_ctr].reshape(rows, width).astype(f32)
    sums = jnp.sum(value_all[:, rows // n_ctr : rows // n_ctr + 6].astype(f32), axis=0)
    norm_now = sums[0] + sums[1] + sums[2]
    curve_ridge = sums[3] + sums[4] + sums[5]

    back_part = dot(kernel_tile, values, ((0,), (0,)))
    back_own = scatter_sum(back_part.reshape(n_pts, cols // n_pts, width), "pts")
    energy_part = jnp.sum(values * values, axis=0)
    extra = jnp.pad(energy_part[None], ((0, 7), (0, 0)))
    back_all = gather(jnp.concatenate([back_own, extra], axis=0), "pts", n_pts)
    back = back_all[:, : cols // n_pts].reshape(cols, width)
    energy = jnp.sum(back_all[:, cols // n_pts], axis=0)

    step_size = norm_now / (energy / total + curve_ridge)
    image = dot(root, back / total + damped, ((1,), (0,)))
    return step_size * spread, gradient - step_size * image


def solution(mesh):
    in_specs = (P("pts", "ctr"), P("ctr", "pts"), P(), P("pts", "ctr"))
    out_specs = (P("ctr", None), P("ctr", None))
    return jax.shard_map(
        on_device, mesh=mesh, in_specs=in_specs, out_specs=out_specs, check_vma=False
    )
```

```python
import math

import jax
import jax.numpy as jnp
from jax import lax
from jax.sharding import Mesh, PartitionSpec as P

BLOCK = 512
ridge_weight = 0.05
jitter_term = 0.1
f32, bf16 = jnp.float32, jnp.bfloat16
high = lax.Precision.HIGH
SPLIT = (("zl", 2), ("y", 8), ("core", 2), ("zh", 4), ("x", 4))
PTS, CTR, COLS = ("zl", "y", "core"), ("zh", "x"), ("zl", "core")


def dot(left, right, dims, precision=high):
    return lax.dot_general(
        left, right, (dims, ((), ())), precision=precision, preferred_element_type=f32
    )


def exchange(parts, axes):
    return lax.all_to_all(parts, axes, 0, 0)


def gather(part, axes, count):
    return exchange(jnp.broadcast_to(part[None], (count,) + part.shape), axes)


def scatter_sum(parts, axes):
    return jnp.sum(exchange(parts, axes).astype(f32), axis=0)


def split(value):
    first = lax.reduce_precision(value, 8, 7)
    rest = value - first
    second = lax.reduce_precision(rest, 8, 7)
    return [t.astype(bf16) for t in (first, second, rest - second)]


def on_device(points, centres, precisions, targets):
    n_y, n_cols, n_ctr = lax.axis_size("y"), 4, 16
    n_pts = n_y * n_cols
    rows, cols, feats = points.shape[0], centres.shape[0], points.shape[1] * n_ctr
    width = targets.shape[1] * n_ctr
    total = rows * n_pts
    group = width // n_cols

    part_feats = points.shape[1]
    both = gather(jnp.concatenate([points.T, targets.T], axis=0), CTR, n_ctr)
    some_centres = gather(centres.T, "y", n_y).reshape(-1, rows)
    half = some_centres.shape[0]
    own_points = both[:, :part_feats].reshape(feats, rows)
    own_targets = both[:, part_feats:].reshape(n_cols, group, rows)
    fixed = jnp.concatenate([own_points, some_centres], axis=0)
    sent = jnp.concatenate(
        [jnp.broadcast_to(fixed[None], (n_cols,) + fixed.shape), own_targets], axis=1
    )
    got = exchange(sent, COLS)
    points_t = got[:, :feats]
    centres_t = got[:, feats : feats + half].reshape(2, 2, n_y, -1, cols)
    centres_t = jnp.swapaxes(centres_t, 1, 2).reshape(feats, cols)
    targets_t = got[:, feats + half :]

    weight = precisions[:, None]
    centre_float = centres_t.astype(f32)
    centre_square = jnp.sum(weight * centre_float * centre_float, axis=0)
    scaled_centres = (centre_float * weight).astype(bf16)
    point_float = points_t.astype(f32)
    point_square = jnp.sum(weight * point_float * point_float, axis=1)
    scaled_points = (point_float * weight).astype(bf16)

    cross_term = jnp.einsum(
        "tfp,fc->tpc", scaled_points, centres_t, preferred_element_type=f32
    )
    kernel_tile = jnp.exp(-(point_square[:, :, None] + centre_square - 2.0 * cross_term))
    right_part = jnp.einsum(
        "tqp,tpc->qc", targets_t.astype(f32), kernel_tile, precision=high
    )
    kernel_tile = kernel_tile.reshape(n_cols * rows, cols)
    right = scatter_sum(right_part.reshape(n_y, group // n_y, cols), "y") / math.sqrt(total)

    forward = dot(scaled_centres, centres_t, ((0,), (0,)), None)
    swapped = dot(centres_t, scaled_centres, ((0,), (0,)), None)
    squares = centre_square[:, None] + centre_square[None, :]
    identity = jnp.eye(BLOCK, dtype=f32)
    blocks = (
        0.5 * (jnp.exp(-(squares - 2.0 * forward)) + jnp.exp(-(squares - 2.0 * swapped)))
        + jitter_term * identity
    )
    scale = jnp.sqrt(jnp.sum(blocks * blocks))
    first = blocks / scale
    second = dot(first, first, ((1,), (0,)))
    inner = 0.0625 * second - 0.5625 * first
    root = (
        2.25 * identity - 2.4375 * first + 1.6875 * second + dot(second, inner, ((1,), (0,)))
    )

    gradient = dot(right, root, ((1,), (0,)))
    spread = dot(gradient, root, ((1,), (0,)))
    damped = ridge_weight * dot(spread, blocks, ((1,), (0,)))
    spread_all = gather(spread, "y", n_y).reshape(group, cols)
    norm_part = jnp.sum(gradient * gradient, axis=1)
    curve_part = jnp.sum(spread * damped, axis=1)

    value_part = dot(spread_all, kernel_tile, ((1,), (1,))).astype(bf16)
    value_own = scatter_sum(value_part.reshape(n_ctr, group // n_ctr, -1), CTR).astype(bf16)
    sums = jnp.concatenate(split(jnp.concatenate([norm_part, curve_part])))
    n_sums = sums.shape[0]
    sums = jnp.broadcast_to(jnp.pad(sums, (0, 128 - n_sums))[None], (group // n_ctr, 128))
    value_all = gather(jnp.concatenate([value_own, sums], axis=1), CTR, n_ctr)
    values = value_all[:, :, :-128].reshape(group, -1).astype(f32)
    sums = jnp.sum(value_all[:, 0, -128:].astype(f32), axis=0)[:n_sums]
    sums = jnp.sum(sums.reshape(3, 2, -1), axis=0)
    norm_now, curve_ridge = sums[0], sums[1]

    back_part = dot(values, kernel_tile, ((1,), (0,)))
    energy_part = jnp.sum(values * values, axis=1, keepdims=True)
    back_part = jnp.concatenate(
        [back_part, jnp.broadcast_to(energy_part, (group, 128))], axis=1
    )
    back = scatter_sum(back_part.reshape(n_y, group // n_y, -1), "y") / total
    step_size = norm_now[:, None] / (back[:, -128:-127] + curve_ridge[:, None])
    image = dot(back[:, :-128] + damped, root, ((1,), (0,)))
    own = jnp.concatenate([step_size * spread, gradient - step_size * image], axis=0)
    every = gather(own, COLS + ("y",), n_pts).reshape(n_pts, 2, -1, cols)
    every = jnp.transpose(every, (1, 3, 0, 2)).reshape(2, cols, width)
    return every[0], every[1]


def solution(mesh):
    names, sizes = zip(*SPLIT)
    fine = Mesh(mesh.devices.reshape(sizes), names)
    in_specs = (P(PTS, CTR), P(CTR, PTS), P(), P(PTS, CTR))
    out_specs = (P(CTR, None), P(CTR, None))
    return jax.shard_map(
        on_device, mesh=fine, in_specs=in_specs, out_specs=out_specs, check_vma=False
    )
```

```python
import math

import jax
import jax.numpy as jnp
from jax import lax
from jax.sharding import Mesh, PartitionSpec as P

BLOCK = 512
ridge_weight = 0.05
jitter_term = 0.1
f32, bf16 = jnp.float32, jnp.bfloat16
high = lax.Precision.HIGH
SPLIT = (("zl", 2), ("y", 8), ("core", 2), ("zh", 4), ("x", 4))
PTS, CTR, COLS = ("zl", "y", "core"), ("zh", "x"), ("zl", "core")


def dot(left, right, dims, precision=high):
    return lax.dot_general(
        left, right, (dims, ((), ())), precision=precision, preferred_element_type=f32
    )


def exchange(parts, axes):
    return lax.all_to_all(parts, axes, 0, 0)


def gather(part, axes, count):
    return exchange(jnp.broadcast_to(part[None], (count,) + part.shape), axes)


def swap(part, axis):
    return lax.ppermute(part, axis, [(0, 1), (1, 0)])


def scatter_sum(parts, axes):
    return jnp.sum(exchange(parts, axes).astype(f32), axis=0)


def split(value):
    first = lax.reduce_precision(value, 8, 7)
    rest = value - first
    second = lax.reduce_precision(rest, 8, 7)
    return [t.astype(bf16) for t in (first, second, rest - second)]


def on_device(points, centres, precisions, targets):
    n_y, n_cols, n_ctr = lax.axis_size("y"), 4, 16
    n_pts = n_y * n_cols
    rows, cols, feats = points.shape[0], centres.shape[0], points.shape[1] * n_ctr
    width = targets.shape[1] * n_ctr
    total = rows * n_pts
    group = width // n_cols

    part_feats = points.shape[1]
    zl, core = lax.axis_index("zl"), lax.axis_index("core")
    own_centres = centres.T
    peer_centres = swap(own_centres, "zl")
    pair = jnp.where(
        zl == 0, jnp.stack([own_centres, peer_centres]), jnp.stack([peer_centres, own_centres])
    )
    both = gather(jnp.concatenate([points.T, targets.T], axis=0), CTR, n_ctr)
    own_points = both[:, :part_feats].reshape(feats, rows)
    own_targets = both[:, part_feats:].reshape(2, 2 * group, rows)
    kept, given = jnp.where(zl == 0, own_targets, own_targets[::-1])
    near = jnp.concatenate([own_points, kept], axis=0)
    far = swap(jnp.concatenate([own_points, given], axis=0), "zl")
    near = jnp.stack([near, far])
    near_points = near[:, :feats]
    near_targets = near[:, feats:].reshape(2, 2, group, rows)
    near_targets = jnp.where(core == 0, near_targets, near_targets[:, ::-1])
    half = gather(pair, "y", n_y).reshape(-1, rows)
    sent = jnp.concatenate(
        [near_points.reshape(-1, rows), near_targets[:, 1].reshape(-1, rows), half], axis=0
    )
    got = swap(sent, "core")
    n_points, n_targets = 2 * feats, 2 * group
    points_t = jnp.concatenate([near_points, got[:n_points].reshape(2, feats, rows)], axis=0)
    targets_t = jnp.concatenate(
        [near_targets[:, 0], got[n_points : n_points + n_targets].reshape(2, group, rows)], axis=0
    )
    half = half.reshape(n_y, 2, -1, cols)
    other = got[n_points + n_targets :].reshape(half.shape)
    centres_t = jnp.where(core == 0, jnp.stack([half, other], 2), jnp.stack([other, half], 2))
    centres_t = jnp.swapaxes(centres_t, 0, 1).reshape(feats, cols)

    weight = precisions[:, None]
    centre_float = centres_t.astype(f32)
    centre_square = jnp.sum(weight * centre_float * centre_float, axis=0)
    scaled_centres = (centre_float * weight).astype(bf16)
    point_float = points_t.astype(f32)
    point_square = jnp.sum(weight * point_float * point_float, axis=1)
    scaled_points = (point_float * weight).astype(bf16)

    cross_term = jnp.einsum(
        "tfp,fc->tpc", scaled_points, centres_t, preferred_element_type=f32
    )
    kernel_tile = jnp.exp(-(point_square[:, :, None] + centre_square - 2.0 * cross_term))
    right_part = jnp.einsum(
        "tqp,tpc->qc", targets_t.astype(f32), kernel_tile, precision=high
    )
    kernel_tile = kernel_tile.reshape(n_cols * rows, cols)
    right = scatter_sum(right_part.reshape(n_y, group // n_y, cols), "y") / math.sqrt(total)

    scaled_centres, centres_t, _ = lax.optimization_barrier(
        (scaled_centres, centres_t, right_part)
    )
    forward = dot(scaled_centres, centres_t, ((0,), (0,)), None)
    swapped = dot(centres_t, scaled_centres, ((0,), (0,)), None)
    squares = centre_square[:, None] + centre_square[None, :]
    identity = jnp.eye(BLOCK, dtype=f32)
    blocks = (
        0.5 * (jnp.exp(-(squares - 2.0 * forward)) + jnp.exp(-(squares - 2.0 * swapped)))
        + jitter_term * identity
    )
    scale = jnp.sqrt(jnp.sum(blocks * blocks))
    first = blocks / scale
    second = dot(first, first, ((1,), (0,)))
    inner = 0.0625 * second - 0.5625 * first
    root = (
        2.25 * identity - 2.4375 * first + 1.6875 * second + dot(second, inner, ((1,), (0,)))
    )

    gradient = dot(right, root, ((1,), (0,)))
    spread = dot(gradient, root, ((1,), (0,)))
    damped = ridge_weight * dot(spread, blocks, ((1,), (0,)))
    spread_all = gather(spread, "y", n_y).reshape(group, cols)
    norm_part = jnp.sum(gradient * gradient, axis=1)
    curve_part = jnp.sum(spread * damped, axis=1)

    value_part = dot(spread_all, kernel_tile, ((1,), (1,))).astype(bf16)
    value_own = scatter_sum(value_part.reshape(n_ctr, group // n_ctr, -1), CTR).astype(bf16)
    sums = jnp.concatenate(split(jnp.concatenate([norm_part, curve_part])))
    n_sums = sums.shape[0]
    sums = jnp.broadcast_to(jnp.pad(sums, (0, 128 - n_sums))[None], (group // n_ctr, 128))
    value_all = gather(jnp.concatenate([value_own, sums], axis=1), CTR, n_ctr)
    values = value_all[:, :, :-128].reshape(group, -1).astype(f32)
    sums = jnp.sum(value_all[:, 0, -128:].astype(f32), axis=0)[:n_sums]
    sums = jnp.sum(sums.reshape(3, 2, -1), axis=0)
    norm_now, curve_ridge = sums[0], sums[1]

    back_part = dot(values, kernel_tile, ((1,), (0,)))
    energy_part = jnp.sum(values * values, axis=1, keepdims=True)
    back_part = jnp.concatenate(
        [back_part, jnp.broadcast_to(energy_part, (group, 128))], axis=1
    )
    back = scatter_sum(back_part.reshape(n_y, group // n_y, -1), "y") / total
    step_size = norm_now[:, None] / (back[:, -128:-127] + curve_ridge[:, None])
    image = dot(back[:, :-128] + damped, root, ((1,), (0,)))
    own = jnp.concatenate([step_size * spread, gradient - step_size * image], axis=0)
    every = gather(own.astype(bf16), COLS + ("y",), n_pts).reshape(2 * width, cols)
    share = width // n_pts
    source = lax.broadcasted_iota(jnp.int32, (2 * width, 2 * width), 0)
    target = lax.broadcasted_iota(jnp.int32, (2 * width, 2 * width), 1)
    place = (source // share % 2) * width + source // (2 * share) * share + source % share
    select = (place == target).astype(bf16)
    every = dot(every, select, ((0,), (0,)), None)
    return every[:, :width], every[:, width:]


def solution(mesh):
    names, sizes = zip(*SPLIT)
    fine = Mesh(mesh.devices.reshape(sizes), names)
    in_specs = (P(PTS, CTR), P(CTR, PTS), P(), P(PTS, CTR))
    out_specs = (P(CTR, None), P(CTR, None))
    return jax.shard_map(
        on_device, mesh=fine, in_specs=in_specs, out_specs=out_specs, check_vma=False
    )
```
